32 devices in a mesh: dp: 8 (over y, x, core), seg: 4 (over z).
Axes of the slice: x: 2, y: 2, z: 4, core: 2. Of those that a mesh axis runs over, the one named last changes fastest.
Arguments:
- tokens: bfloat16 [2, 16, 2048, 768], P(None, 'dp', 'seg'), may hold values from -6 to 6
- cotangent: bfloat16 [2, 16, 2048, 768], P(None, 'dp', 'seg'), may hold values from -6 to 6
- document_ids: int32 [2, 16, 16], P(None, 'dp'), may hold values from 0 to 3, never falling along the last dimension, each value on 1 to 8 neighbouring positions
- position_ids: int32 [2, 16, 16], P(None, 'dp'), may hold values from 0 to 63
- project_in: bfloat16 [2, 768, 2304], P(None, 'dp', 'seg'), may hold values from -0.3125 to 0.3125
- project_out: bfloat16 [2, 768, 768], P(None, 'dp', 'seg'), may hold values from -0.875 to 0.875
- up_weight: bfloat16 [2, 768, 3072], P(None, 'dp', 'seg'), may hold values from -0.21875 to 0.21875
- down_weight: bfloat16 [2, 3072, 768], P(None, 'dp', 'seg'), may hold values from -0.109375 to 0.109375
- norm_gains: bfloat16 [2, 768, 2], P(None, 'dp'), may hold values from 0.5 to 1.5
- biases: bfloat16 [2, 768, 6], P(None, 'dp'), may hold values from -1.25 to 1.25
- up_bias: bfloat16 [2, 3072], P(None, 'dp'), may hold values from -1.25 to 1.25
- position_table: bfloat16 [768, 64], P('dp'), may hold values from -3 to 3
Outputs:
- layer_out: bfloat16 [2, 16, 2048, 768], P(None, 'dp', 'seg')
- input_grad: float32 [2, 16, 2048, 768], P(None, 'dp', 'seg')
- project_in_grad: float32 [2, 768, 2304], P(None, 'dp', 'seg')
- project_out_grad: float32 [2, 768, 768], P(None, 'dp', 'seg')
- up_weight_grad: float32 [2, 768, 3072], P(None, 'dp', 'seg')
- down_weight_grad: float32 [2, 3072, 768], P(None, 'dp', 'seg')
- norm_gains_grad: float32 [2, 768, 2], P(None, 'dp')
- biases_grad: float32 [2, 768, 6], P(None, 'dp')
- up_bias_grad: float32 [2, 3072], P(None, 'dp')
- position_table_grad: float32 [768, 64], P('dp')
The draws below stay inside these ranges and needn't reach their ends.
Inputs may be any that keep to these rules, and one draw needn't show every extreme that they name: `document_ids`: document ids count from 0 in every row and never fall along it; a document has 1 to 8 segments.
All inputs are finite; a program needn't handle non-finite values.
Results may differ from the reference program's by a relative error of at most 0.028.
Values may be sent and summed in bfloat16 or wider, within the bound.
A program may use at most 320 MiB of HBM per device.

```python
import math
import jax
import jax.numpy as jnp
import numpy as np
from jax import lax

D = 768
HEADS = 12
HD = 64
FF = 3072
SEGLEN = 128
POS = 64
MB = 2
ROWS = 16
SEG_ROW = 16
TOKS_ROW = 2048


def plant(entries, rng, low, high):
    place = [jax.random.randint(jax.random.fold_in(rng, axis), (), 0, length) for axis, length in enumerate(entries.shape)]
    widest = entries.shape.index(max(entries.shape))
    neighbour = place[:widest] + [(place[widest] + 1) % entries.shape[widest]] + place[widest + 1:]
    return entries.at[tuple(place)].set(low).at[tuple(neighbour)].set(high)


def block_levels(rng, extent, pieces, smallest, top_value):
    def one(axis_at, blocks):
        steps = jax.random.uniform(jax.random.fold_in(jax.random.fold_in(rng, 6), axis_at), (blocks,), jnp.float32, smallest / len(pieces), top_value / len(pieces))
        return jnp.repeat(jnp.exp(steps), extent[axis_at] // blocks).reshape((-1,) + (1,) * (len(extent) - axis_at - 1))

    loudness = one(*pieces[0])
    for cut in pieces[1:]:
        loudness = loudness * one(*cut)
    return loudness


def profile(number_of, total, reach, skew):
    weights = [(1 << 20) // math.isqrt(standing ** skew) + 1 for standing in range(2, number_of + 1)]
    rest, given = total - reach - (number_of - 1), [1] * (number_of - 1)
    while rest > 0:
        free = [i for i in range(number_of - 1) if given[i] < reach]
        mass, remaining = sum([weights[i] for i in free]), rest
        for i in free:
            addition = min(reach - given[i], max(1, remaining * weights[i] // mass), rest)
            given[i] = given[i] + addition
            rest = rest - addition
    return np.array([reach] + given)


def ragged_sizes(rng, amount, total, reach, lean):
    if amount == 2:
        one = jax.random.randint(rng, (), max(1, total - reach), min(reach, total - 1) + 1)
        return jnp.stack([one, total - one])
    sizes = jnp.asarray(profile(amount, total, reach, lean), jnp.int32)
    pairs = (amount - 1) // 2
    giver, taker = sizes[1:1 + 2 * pairs:2], sizes[2:2 + 2 * pairs:2]
    slack = jnp.minimum(giver - 1, reach - taker)
    moved = jax.random.randint(jax.random.fold_in(rng, 1), (pairs,), 0, 1 << 20) % (slack + 1)
    sizes = sizes.at[1:1 + 2 * pairs:2].set(giver - moved).at[2:2 + 2 * pairs:2].set(taker + moved)
    return sizes[jax.random.permutation(jax.random.fold_in(rng, 2), amount)]


def scatter_about(stream_key, shape, width, most, shards=(), kind=jnp.bfloat16):
    values = width * jax.random.normal(stream_key, shape, jnp.float32)
    if shards:
        values = values * block_levels(stream_key, shape, shards, -0.22, 0.18)
    return jnp.clip(values, -most, most).astype(kind)


def setup_inputs(seed: int = 0) -> dict:
    key_of = jax.random.split(jax.random.key(seed), 13)
    return {
        "tokens": scatter_about(key_of[0], (MB, ROWS, TOKS_ROW, D), 1.0, 6.0, ((1, 8), (2, 4))),
        "cotangent": scatter_about(key_of[1], (MB, ROWS, TOKS_ROW, D), 1.0, 6.0, ((1, 8), (2, 4))),
        "document_ids": jax.vmap(lambda own: jnp.searchsorted(jnp.cumsum(ragged_sizes(own, 4, SEG_ROW, SEG_ROW // 2, 0)), jnp.arange(SEG_ROW), side="right"))(jax.random.split(key_of[2], MB * ROWS)).reshape((MB, ROWS, SEG_ROW)).astype(jnp.int32),
        "position_ids": plant(jax.random.randint(key_of[3], (MB, ROWS, SEG_ROW), 0, POS), jax.random.fold_in(key_of[3], 1), 0, POS - 1).astype(jnp.int32),
        "project_in": scatter_about(key_of[4], (2, D, 3 * D), (D // 2) ** -0.5, 0.3125, ((1, 8), (2, 4))),
        "project_out": scatter_about(key_of[5], (2, D, D), (D // 16) ** -0.5, 0.875, ((1, 8), (2, 4))),
        "up_weight": scatter_about(key_of[6], (2, D, FF), D ** -0.5, 0.21875, ((1, 8), (2, 4))),
        "down_weight": scatter_about(key_of[7], (2, FF, D), FF ** -0.5, 0.109375, ((1, 8), (2, 4))),
        "norm_gains": jnp.clip(1.0 + 0.1 * jax.random.normal(key_of[8], (2, D, 2), jnp.float32), 0.5, 1.5).astype(jnp.bfloat16),
        "biases": scatter_about(key_of[9], (2, D, 6), 0.2, 1.25, ((1, 8),)),
        "up_bias": scatter_about(key_of[10], (2, FF), 0.2, 1.25, ((1, 8),)),
        "position_table": scatter_about(key_of[11], (D, POS), 0.5, 3.0, ((0, 8),)),
    }


NORM_EPS = 1e-05
PRECISE = lax.Precision.HIGHEST

@jax.custom_vjp
def low(v):
    return lax.optimization_barrier(v.astype(jnp.bfloat16)).astype(jnp.float32)

@jax.custom_vjp
def low_back(v):
    return v

def low_keep(v):
    return (low(v), None)

def low_pass(kept, grad):
    return (grad,)

def back_keep(v):
    return (v, None)

def back_low(kept, grad):
    return (low(grad),)
low.defvjp(low_keep, low_pass)
low_back.defvjp(back_keep, back_low)

def norm_apply(inputs, norm_gain, norm_shift):
    average = lax.optimization_barrier(jnp.mean(inputs, axis=-1, keepdims=True))
    centered = inputs - average
    variance = lax.optimization_barrier(jnp.mean(centered * centered, axis=-1, keepdims=True))
    return centered * lax.rsqrt(variance + NORM_EPS) * norm_gain + norm_shift

def attend(queries, key_rows, values, same_document):
    scores = low_back(jnp.einsum('gqhe,gkhe->ghqk', queries, key_rows, precision=PRECISE) * HD ** (-0.5))
    if same_document is not None:
        scores = jnp.where(same_document[:, None, :, :], scores, -1e+30)
    attention = jnp.exp(scores - jax.nn.logsumexp(scores, axis=-1, keepdims=True))
    return jnp.einsum('ghqk,gkhe->gqhe', low(attention), values, precision=PRECISE)

def layer_block(inputs, project_in, project_out, up_weight, down_weight, norm_gains, biases, up_bias, same_document):
    features = inputs.shape[-1]
    leading = inputs.shape[:-1]
    head_shape = leading + (HEADS, HD)
    source = low(inputs)
    joined = jnp.einsum('gld,de->gle', source, project_in, precision=PRECISE)
    queries = low_back(low(joined[..., :features] + biases[:, 0]))
    key_rows = low_back(low(joined[..., features:2 * features]))
    values = low_back(low(joined[..., 2 * features:] + biases[:, 1]))
    context = attend(queries.reshape(head_shape), key_rows.reshape(head_shape), values.reshape(head_shape), same_document)
    context = low_back(low(context.reshape(leading + (features,))))
    mixed = low_back(jnp.einsum('gld,de->gle', context, project_out, precision=PRECISE) + biases[:, 2])
    first_norm = norm_apply(inputs + mixed, norm_gains[:, 0], biases[:, 4])
    pre_gelu = low_back(jnp.einsum('gld,df->glf', low(first_norm), up_weight, precision=PRECISE) + up_bias)
    activation = low(jax.nn.gelu(pre_gelu, approximate=False))
    branch = low_back(jnp.einsum('glf,fd->gld', activation, down_weight, precision=PRECISE) + biases[:, 3])
    return norm_apply(first_norm + branch, norm_gains[:, 1], biases[:, 5])

def row_forward(params, row_tokens, row_positions, row_documents):
    project_in, project_out, up_weight, down_weight, norm_gains, biases, up_bias, position_table = params
    segments = row_tokens.reshape(SEG_ROW, SEGLEN, D)
    local_out = layer_block(segments, project_in[0], project_out[0], up_weight[0], down_weight[0], norm_gains[0], biases[0], up_bias[0], None)
    class_rows = low(local_out[:, 0, :])
    one_hot = (row_positions[:, None] == jnp.arange(POS, dtype=jnp.int32)[None, :]).astype(jnp.float32)
    cross_in = class_rows + jnp.dot(one_hot, position_table.T, precision=PRECISE)
    same_document = row_documents[:, None] == row_documents[None, :]
    cross_out = layer_block(cross_in[None], project_in[1], project_out[1], up_weight[1], down_weight[1], norm_gains[1], biases[1], up_bias[1], same_document[None])[0]
    merged = local_out.at[:, 0, :].set(cross_out)
    return merged.reshape(SEG_ROW * SEGLEN, D)

def reference(tokens, cotangent, document_ids, position_ids, project_in, project_out, up_weight, down_weight, norm_gains, biases, up_bias, position_table):
    params = tuple((member.astype(jnp.float32) for member in (project_in, project_out, up_weight, down_weight, norm_gains, biases, up_bias, position_table)))
    row_total = MB * ROWS
    flat_tokens = tokens.reshape(row_total, SEG_ROW * SEGLEN, D).astype(jnp.float32)
    flat_grads = cotangent.reshape(row_total, SEG_ROW * SEGLEN, D).astype(jnp.float32)
    flat_positions = position_ids.reshape(row_total, SEG_ROW)
    flat_documents = document_ids.reshape(row_total, SEG_ROW)

    def one_row(totals, row_items):
        row_tokens, row_grad, row_positions, row_documents = row_items

        def forward(weights, inputs):
            return row_forward(weights, inputs, row_positions, row_documents)
        result, pull_back = jax.vjp(forward, params, row_tokens)
        weight_grads, token_grad = pull_back(row_grad)
        totals = jax.tree.map(jnp.add, totals, weight_grads)
        return (totals, (result.astype(jnp.bfloat16), token_grad))
    zero_totals = jax.tree.map(jnp.zeros_like, params)
    totals, (outputs, token_grads) = lax.scan(one_row, zero_totals, (flat_tokens, flat_grads, flat_positions, flat_documents))
    return (outputs.reshape(tokens.shape), token_grads.reshape(tokens.shape), totals[0], totals[1], totals[2], totals[3], totals[4], totals[5], totals[6], totals[7])
```

```python
import jax
import jax.numpy as jnp
from jax import lax
from jax.sharding import PartitionSpec as P

HEADS = 12
HD = 64
SEGLEN = 128
POS = 64


NORM_EPS = 1e-05
PRECISE = lax.Precision.HIGHEST


def norm_apply(inputs, norm_gain, norm_shift):
    average = jnp.mean(inputs, axis=-1, keepdims=True)
    centered = inputs - average
    variance = jnp.mean(centered * centered, axis=-1, keepdims=True)
    return centered * lax.rsqrt(variance + NORM_EPS) * norm_gain + norm_shift


def norm_backward(inputs, norm_gain, norm_shift, upstream):
    unused_out, pull_back = jax.vjp(norm_apply, inputs, norm_gain, norm_shift)
    return pull_back(upstream)


def gelu_exact(inputs):
    return jax.nn.gelu(inputs, approximate=False)


def soft_scores(queries, key_rows, same_document):
    scores = jnp.einsum(
        "gqhe,gkhe->ghqk", queries, key_rows, preferred_element_type=jnp.float32
    ) * HD ** (-0.5)
    if same_document is not None:
        scores = jnp.where(same_document[:, None, :, :], scores, -1e30)
    return scores


def block_forward(source, residual, weights, same_document):
    project_in, project_out, up_weight, down_weight, norm_gains, biases, up_bias = weights
    features = source.shape[-1]
    leading = source.shape[:-1]
    head_shape = leading + (HEADS, HD)
    joined = jnp.einsum("gld,de->gle", source, project_in, preferred_element_type=jnp.float32)
    queries = (joined[..., :features] + biases[:, 0]).astype(jnp.bfloat16)
    key_rows = joined[..., features : 2 * features].astype(jnp.bfloat16)
    values = (joined[..., 2 * features :] + biases[:, 1]).astype(jnp.bfloat16)
    scores = soft_scores(queries.reshape(head_shape), key_rows.reshape(head_shape), same_document)
    log_total = jax.nn.logsumexp(scores, axis=-1, keepdims=True)
    attention = jnp.exp(scores - log_total).astype(jnp.bfloat16)
    context = jnp.einsum(
        "ghqk,gkhe->gqhe", attention, values.reshape(head_shape), preferred_element_type=jnp.float32
    )
    context = context.reshape(leading + (features,)).astype(jnp.bfloat16)
    mixed_input = residual + (
        jnp.einsum("gld,de->gle", context, project_out, preferred_element_type=jnp.float32)
        + biases[:, 2]
    )
    first_norm = norm_apply(mixed_input, norm_gains[:, 0], biases[:, 4])
    first_low = first_norm.astype(jnp.bfloat16)
    pre_gelu = (
        jnp.einsum("gld,df->glf", first_low, up_weight, preferred_element_type=jnp.float32)
        + up_bias
    )
    activation = gelu_exact(pre_gelu).astype(jnp.bfloat16)
    second_input = first_norm + (
        jnp.einsum("glf,fd->gld", activation, down_weight, preferred_element_type=jnp.float32)
        + biases[:, 3]
    )
    result = norm_apply(second_input, norm_gains[:, 1], biases[:, 5])
    stored = (
        queries,
        key_rows,
        values,
        log_total,
        context,
        mixed_input,
        first_low,
        pre_gelu,
        activation,
        second_input,
    )
    return (result, stored)


def block_backward(source, stored, weights, same_document, upstream, pick):
    project_in, project_out, up_weight, down_weight, norm_gains, biases, up_bias = weights
    (
        queries,
        key_rows,
        values,
        log_total,
        context,
        mixed_input,
        first_low,
        pre_gelu,
        activation,
        second_input,
    ) = stored
    features = source.shape[-1]
    leading = source.shape[:-1]
    head_shape = leading + (HEADS, HD)
    sum_axes = (0, 1)
    second_grad, gain_two, shift_two = norm_backward(
        second_input, norm_gains[:, 1], biases[:, 5], upstream
    )
    branch_grad = second_grad.astype(jnp.bfloat16)
    down_grad = jnp.einsum(
        "glf,gld->fd", activation, pick(branch_grad), preferred_element_type=jnp.float32
    )
    activation_grad = jnp.einsum(
        "gld,fd->glf", branch_grad, down_weight, preferred_element_type=jnp.float32
    )
    unused_out, gelu_pull = jax.vjp(gelu_exact, pre_gelu)
    pre_gelu_grad = gelu_pull(activation_grad)[0].astype(jnp.bfloat16)
    up_grad = jnp.einsum(
        "gld,glf->df", first_low, pick(pre_gelu_grad), preferred_element_type=jnp.float32
    )
    first_grad = second_grad + jnp.einsum(
        "glf,df->gld", pre_gelu_grad, up_weight, preferred_element_type=jnp.float32
    )
    mixed_grad, gain_one, shift_one = norm_backward(
        mixed_input, norm_gains[:, 0], biases[:, 4], first_grad
    )
    mixed_low = mixed_grad.astype(jnp.bfloat16)
    outward_grad = jnp.einsum("gld,gle->de", context, pick(mixed_low), preferred_element_type=jnp.float32)
    context_grad = jnp.einsum(
        "gle,de->gld", mixed_low, project_out, preferred_element_type=jnp.float32
    )
    context_grad = context_grad.astype(jnp.bfloat16).reshape(head_shape)
    query_heads = queries.reshape(head_shape)
    key_heads = key_rows.reshape(head_shape)
    scores = soft_scores(query_heads, key_heads, same_document)
    attention = jnp.exp(scores - log_total)
    value_grad = jnp.einsum(
        "ghqk,gqhe->gkhe",
        attention.astype(jnp.bfloat16),
        context_grad,
        preferred_element_type=jnp.float32,
    )
    soft_grad = jnp.einsum(
        "gqhe,gkhe->ghqk",
        context_grad,
        values.reshape(head_shape),
        preferred_element_type=jnp.float32,
    )
    score_grad = attention * (soft_grad - jnp.sum(soft_grad * attention, axis=-1, keepdims=True))
    score_grad = score_grad.astype(jnp.bfloat16)
    query_grad = jnp.einsum(
        "ghqk,gkhe->gqhe", score_grad, key_heads, preferred_element_type=jnp.float32
    ) * HD ** (-0.5)
    key_grad = jnp.einsum(
        "ghqk,gqhe->gkhe", score_grad, query_heads, preferred_element_type=jnp.float32
    ) * HD ** (-0.5)
    joined_grad = jnp.concatenate(
        [
            query_grad.reshape(leading + (features,)),
            key_grad.reshape(leading + (features,)),
            value_grad.reshape(leading + (features,)),
        ],
        axis=-1,
    ).astype(jnp.bfloat16)
    inward_grad = jnp.einsum("gld,gle->de", source, pick(joined_grad), preferred_element_type=jnp.float32)
    source_grad = mixed_grad + jnp.einsum(
        "gle,de->gld", joined_grad, project_in, preferred_element_type=jnp.float32
    )
    bias_grad = jnp.stack(
        [
            jnp.sum(joined_grad[..., :features], axis=sum_axes, dtype=jnp.float32),
            jnp.sum(joined_grad[..., 2 * features :], axis=sum_axes, dtype=jnp.float32),
            jnp.sum(mixed_low, axis=sum_axes, dtype=jnp.float32),
            jnp.sum(branch_grad, axis=sum_axes, dtype=jnp.float32),
            shift_one,
            shift_two,
        ],
        axis=-1,
    )
    gain_grad = jnp.stack([gain_one, gain_two], axis=-1)
    bias_up_grad = jnp.sum(pre_gelu_grad, axis=sum_axes, dtype=jnp.float32)
    return (
        source_grad,
        (inward_grad, outward_grad, up_grad, down_grad, gain_grad, bias_grad, bias_up_grad),
    )


def gather_matrix(pieces):
    joined = jnp.concatenate(pieces, axis=1) if len(pieces) > 1 else pieces[0]
    full = lax.all_gather(joined, ("seg", "dp"), axis=0, tiled=False)
    seg = lax.axis_size("seg")
    return full.reshape(seg, -1, joined.shape[1])


def unfold(part):
    return part.transpose(1, 0, 2).reshape(part.shape[1], -1)


def gather_block(project_in, project_out, up_weight, down_weight):
    rows, wide = up_weight.shape
    down_packed = down_weight.reshape(rows, -1)
    first = gather_matrix([project_in, project_out])
    second = gather_matrix([up_weight])
    third = gather_matrix([down_packed])
    seg = third.shape[0]
    down_full = third.reshape(seg, -1, down_weight.shape[1])
    cut = project_in.shape[1]
    return (
        unfold(first[:, :, :cut]),
        unfold(first[:, :, cut:]),
        unfold(second),
        unfold(down_full),
    )


def own_columns(array, shard_index, seg):
    width = array.shape[-1] // seg
    return lax.dynamic_slice_in_dim(array, shard_index * width, width, array.ndim - 1)


def reduce_rows(array):
    return lax.psum_scatter(array.astype(jnp.bfloat16), "dp", scatter_dimension=0, tiled=True)


def reduce_columns(array):
    return lax.psum_scatter(array, "seg", scatter_dimension=1, tiled=True).astype(jnp.float32)


def shards(
    tokens,
    cotangent,
    document_ids,
    position_ids,
    project_in,
    project_out,
    up_weight,
    down_weight,
    norm_gains,
    biases,
    up_bias,
    position_table,
):
    shard_index = lax.axis_index("seg")
    seg = lax.axis_size("seg")
    micro_count, row_count, row_tokens, features = tokens.shape
    segment_count = row_tokens // SEGLEN
    rows = micro_count * row_count
    group_count = rows * segment_count
    own_rows = project_in.shape[1]
    slot_ids = jnp.arange(POS, dtype=jnp.int32)
    up_packed = up_bias.reshape(2, own_rows, -1).transpose(1, 0, 2).reshape(own_rows, -1)
    small = jnp.concatenate(
        [
            norm_gains.transpose(1, 0, 2).reshape(own_rows, 4),
            biases.transpose(1, 0, 2).reshape(own_rows, 12),
            up_packed,
            position_table,
        ],
        axis=1,
    )
    small = lax.all_gather(small, "dp", axis=0, tiled=True)
    many = up_packed.shape[1]
    gains_full = small[:, :4].reshape(features, 2, 2).astype(jnp.float32)
    biases_full = small[:, 4:16].reshape(features, 2, 6).astype(jnp.float32)
    up_full = small[:, 16 : 16 + many].reshape(features, 2, -1).astype(jnp.float32)
    gathered_table = small[:, 16 + many :]

    def weights_of(which):
        return gather_block(
            project_in[which], project_out[which], up_weight[which], down_weight[which]
        ) + (
            gains_full[:, which],
            biases_full[:, which],
            up_full[:, which].reshape(-1),
        )

    local_weights = weights_of(0)
    cross_weights = weights_of(1)
    segments = tokens.reshape(group_count, SEGLEN, features)
    local_out, local_stored = block_forward(
        segments, segments.astype(jnp.float32), local_weights, None
    )
    class_own = local_out[:, 0, :].astype(jnp.bfloat16).reshape(rows, segment_count, features)
    upstream = cotangent.reshape(group_count, SEGLEN, features)
    class_grad_own = upstream[:, 0, :].reshape(rows, segment_count, features)
    class_rows = lax.all_gather(class_own, "seg", axis=1, tiled=True)
    class_grads = lax.all_gather(class_grad_own, "seg", axis=1, tiled=True)
    positions = position_ids.reshape(rows, -1)
    one_hot = (positions[:, :, None] == slot_ids).astype(jnp.bfloat16)
    cross_in = class_rows.astype(jnp.float32) + jnp.einsum(
        "rsp,dp->rsd", one_hot, gathered_table, preferred_element_type=jnp.float32
    )
    documents = document_ids.reshape(rows, -1)
    same_document = documents[:, :, None] == documents[:, None, :]
    cross_low = cross_in.astype(jnp.bfloat16)
    cross_out, cross_stored = block_forward(cross_low, cross_in, cross_weights, same_document)
    cross_own = lax.dynamic_slice_in_dim(cross_out, shard_index * segment_count, segment_count, 1)
    merged = local_out.at[:, 0, :].set(cross_own.reshape(group_count, features))
    layer_out = merged.astype(jnp.bfloat16).reshape(tokens.shape)

    def all_columns(array):
        return array

    def mine(array):
        return own_columns(array, shard_index, seg)

    cross_grad, cross_terms = block_backward(
        cross_low, cross_stored, cross_weights, same_document, class_grads.astype(jnp.float32), mine
    )
    table_grad = jnp.einsum("rsd,rsp->dp", cross_grad, one_hot.astype(jnp.float32), precision=PRECISE)
    own_grad = lax.dynamic_slice_in_dim(cross_grad, shard_index * segment_count, segment_count, 1)
    local_upstream = (
        upstream.astype(jnp.float32).at[:, 0, :].set(own_grad.reshape(group_count, features))
    )
    token_grad, local_terms = block_backward(
        segments, local_stored, local_weights, None, local_upstream, all_columns
    )
    input_grad = token_grad.reshape(tokens.shape)
    cross_packed = reduce_rows(
        jnp.concatenate(
            [
                term.astype(jnp.bfloat16).reshape(features, -1)
                for term in (cross_terms[0], cross_terms[1], cross_terms[2], cross_terms[3])
            ],
            axis=1,
        )
    ).astype(jnp.float32)
    widths = [project_in.shape[2], project_out.shape[2], up_weight.shape[2]]
    ends = [widths[0], widths[0] + widths[1], sum(widths)]
    cross_parts = (
        cross_packed[:, : ends[0]],
        cross_packed[:, ends[0] : ends[1]],
        cross_packed[:, ends[1] : ends[2]],
        cross_packed[:, ends[2] :].reshape(down_weight.shape[1:]),
    )
    local_parts = tuple(reduce_columns(reduce_rows(term)) for term in local_terms[:4])
    matrices = tuple(jnp.stack(pair) for pair in zip(local_parts, cross_parts))

    def small_terms(terms):
        return [terms[4], terms[5], terms[6].reshape(features, -1)]

    first_shard = (shard_index == 0).astype(jnp.float32)
    small_grads = jnp.concatenate(
        small_terms(local_terms)
        + [term * first_shard for term in small_terms(cross_terms) + [table_grad]],
        axis=1,
    )
    small_grads = reduce_rows(small_grads).astype(jnp.float32)
    small_grads = jnp.sum(lax.all_gather(small_grads, "seg", axis=0, tiled=False), axis=0)
    half = many // 2
    local_small = small_grads[:, : 8 + half]
    cross_small = small_grads[:, 8 + half : 16 + many]
    pair = jnp.stack([local_small, cross_small])
    return (layer_out, input_grad) + matrices + (
        pair[:, :, :2],
        pair[:, :, 2:8],
        pair[:, :, 8:].reshape(up_bias.shape),
        small_grads[:, 16 + many :],
    )


def solution(mesh):
    placed = (
        P(None, "dp", "seg", None),
        P(None, "dp", "seg", None),
        P(None, "dp", None),
        P(None, "dp", None),
        P(None, "dp", "seg"),
        P(None, "dp", "seg"),
        P(None, "dp", "seg"),
        P(None, "dp", "seg"),
        P(None, "dp", None),
        P(None, "dp", None),
        P(None, "dp"),
        P("dp", None),
    )
    return jax.shard_map(
        shards,
        mesh=mesh,
        in_specs=placed,
        out_specs=(
            P(None, "dp", "seg", None),
            P(None, "dp", "seg", None),
            P(None, "dp", "seg"),
            P(None, "dp", "seg"),
            P(None, "dp", "seg"),
            P(None, "dp", "seg"),
            P(None, "dp", None),
            P(None, "dp", None),
            P(None, "dp"),
            P("dp", None),
        ),
        check_vma=False,
    )
```

```python
import jax
import jax.numpy as jnp
from jax import lax
from jax.sharding import PartitionSpec as P

HEADS = 12
HD = 64
SEGLEN = 128
POS = 64


NORM_EPS = 1e-05
PRECISE = lax.Precision.HIGHEST


def norm_apply(inputs, norm_gain, norm_shift):
    average = jnp.mean(inputs, axis=-1, keepdims=True)
    centered = inputs - average
    variance = jnp.mean(centered * centered, axis=-1, keepdims=True)
    return centered * lax.rsqrt(variance + NORM_EPS) * norm_gain + norm_shift


def norm_backward(inputs, norm_gain, norm_shift, upstream):
    unused_out, pull_back = jax.vjp(norm_apply, inputs, norm_gain, norm_shift)
    return pull_back(upstream)


def gelu_exact(inputs):
    return jax.nn.gelu(inputs, approximate=False)


def soft_scores(queries, key_rows, same_document):
    scores = jnp.einsum(
        "gqhe,gkhe->ghqk", queries, key_rows, preferred_element_type=jnp.float32
    ) * HD ** (-0.5)
    if same_document is not None:
        scores = jnp.where(same_document[:, None, :, :], scores, -1e30)
    return scores


def block_forward(source, residual, weights, same_document):
    project_in, project_out, up_weight, down_weight, norm_gains, biases, up_bias = weights
    features = source.shape[-1]
    leading = source.shape[:-1]
    head_shape = leading + (HEADS, HD)
    joined = jnp.einsum("gld,de->gle", source, project_in, preferred_element_type=jnp.float32)
    queries = (joined[..., :features] + biases[:, 0]).astype(jnp.bfloat16)
    key_rows = joined[..., features : 2 * features].astype(jnp.bfloat16)
    values = (joined[..., 2 * features :] + biases[:, 1]).astype(jnp.bfloat16)
    scores = soft_scores(queries.reshape(head_shape), key_rows.reshape(head_shape), same_document)
    log_total = jax.nn.logsumexp(scores, axis=-1, keepdims=True)
    attention = jnp.exp(scores - log_total).astype(jnp.bfloat16)
    context = jnp.einsum(
        "ghqk,gkhe->gqhe", attention, values.reshape(head_shape), preferred_element_type=jnp.float32
    )
    context = context.reshape(leading + (features,)).astype(jnp.bfloat16)
    mixed_input = residual + (
        jnp.einsum("gld,de->gle", context, project_out, preferred_element_type=jnp.float32)
        + biases[:, 2]
    )
    first_norm = norm_apply(mixed_input, norm_gains[:, 0], biases[:, 4])
    first_low = first_norm.astype(jnp.bfloat16)
    pre_gelu = (
        jnp.einsum("gld,df->glf", first_low, up_weight, preferred_element_type=jnp.float32)
        + up_bias
    )
    activation = gelu_exact(pre_gelu).astype(jnp.bfloat16)
    second_input = first_norm + (
        jnp.einsum("glf,fd->gld", activation, down_weight, preferred_element_type=jnp.float32)
        + biases[:, 3]
    )
    result = norm_apply(second_input, norm_gains[:, 1], biases[:, 5])
    stored = (
        queries,
        key_rows,
        values,
        log_total,
        context,
        mixed_input,
        first_low,
        pre_gelu,
        activation,
        second_input,
    )
    return (result, stored)


def after(value, *earlier):
    return lax.optimization_barrier((value,) + earlier)


def total_over(array, axis_name):
    return jnp.sum(lax.all_gather(array, axis_name, axis=0, tiled=False), axis=0)


def attention_backward(queries, key_rows, values, log_total, same_document, context_grad):
    head_shape = queries.shape[:-1] + (HEADS, HD)
    features = queries.shape[-1]
    leading = queries.shape[:-1]
    context_grad = context_grad.reshape(head_shape)
    query_heads = queries.reshape(head_shape)
    key_heads = key_rows.reshape(head_shape)
    scores = soft_scores(query_heads, key_heads, same_document)
    attention = jnp.exp(scores - log_total)
    value_grad = jnp.einsum(
        "ghqk,gqhe->gkhe",
        attention.astype(jnp.bfloat16),
        context_grad,
        preferred_element_type=jnp.float32,
    )
    soft_grad = jnp.einsum(
        "gqhe,gkhe->ghqk",
        context_grad,
        values.reshape(head_shape),
        preferred_element_type=jnp.float32,
    )
    score_grad = attention * (soft_grad - jnp.sum(soft_grad * attention, axis=-1, keepdims=True))
    score_grad = score_grad.astype(jnp.bfloat16)
    query_grad = jnp.einsum(
        "ghqk,gkhe->gqhe", score_grad, key_heads, preferred_element_type=jnp.float32
    ) * HD ** (-0.5)
    key_grad = jnp.einsum(
        "ghqk,gqhe->gkhe", score_grad, query_heads, preferred_element_type=jnp.float32
    ) * HD ** (-0.5)
    return jnp.concatenate(
        [
            query_grad.reshape(leading + (features,)),
            key_grad.reshape(leading + (features,)),
            value_grad.reshape(leading + (features,)),
        ],
        axis=-1,
    ).astype(jnp.bfloat16)


def local_backward(source, stored, weights, upstream):
    project_in, project_out, up_weight, down_weight, norm_gains, biases, up_bias = weights
    (
        queries,
        key_rows,
        values,
        log_total,
        context,
        mixed_input,
        first_low,
        pre_gelu,
        activation,
        second_input,
    ) = stored
    sum_axes = (0, 1)
    second_grad, gain_two, shift_two = norm_backward(
        second_input, norm_gains[:, 1], biases[:, 5], upstream
    )
    branch_grad = second_grad.astype(jnp.bfloat16)
    down_grad = jnp.einsum(
        "glf,gld->fd", activation, branch_grad, preferred_element_type=jnp.float32
    ).astype(jnp.bfloat16)
    branch_grad, down_grad = after(branch_grad, down_grad)
    activation_grad = jnp.einsum(
        "gld,fd->glf", branch_grad, down_weight, preferred_element_type=jnp.float32
    )
    unused_out, gelu_pull = jax.vjp(gelu_exact, pre_gelu)
    pre_gelu_grad = gelu_pull(activation_grad)[0].astype(jnp.bfloat16)
    up_grad = jnp.einsum(
        "gld,glf->df", first_low, pre_gelu_grad, preferred_element_type=jnp.float32
    ).astype(jnp.bfloat16)
    pre_gelu_grad, up_grad = after(pre_gelu_grad, up_grad)
    first_grad = second_grad + jnp.einsum(
        "glf,df->gld", pre_gelu_grad, up_weight, preferred_element_type=jnp.float32
    )
    mixed_grad, gain_one, shift_one = norm_backward(
        mixed_input, norm_gains[:, 0], biases[:, 4], first_grad
    )
    mixed_low = mixed_grad.astype(jnp.bfloat16)
    outward_grad = jnp.einsum(
        "gld,gle->de", context, mixed_low, preferred_element_type=jnp.float32
    ).astype(jnp.bfloat16)
    mixed_low, outward_grad = after(mixed_low, outward_grad)
    context_grad = jnp.einsum(
        "gle,de->gld", mixed_low, project_out, preferred_element_type=jnp.float32
    ).astype(jnp.bfloat16)
    joined_grad = attention_backward(queries, key_rows, values, log_total, None, context_grad)
    inward_grad = jnp.einsum(
        "gld,gle->de", source, joined_grad, preferred_element_type=jnp.float32
    ).astype(jnp.bfloat16)
    joined_grad, inward_grad = after(joined_grad, inward_grad)
    source_grad = mixed_grad + jnp.einsum(
        "gle,de->gld", joined_grad, project_in, preferred_element_type=jnp.float32
    )
    sums = jnp.sum(joined_grad, axis=sum_axes, dtype=jnp.float32)
    width = source.shape[-1]
    late = jnp.stack([sums[:width], sums[2 * width :]], axis=-1)
    early = jnp.stack(
        [
            jnp.sum(mixed_low, axis=sum_axes, dtype=jnp.float32),
            jnp.sum(branch_grad, axis=sum_axes, dtype=jnp.float32),
            shift_one,
            shift_two,
            gain_one,
            gain_two,
        ],
        axis=-1,
    )
    bias_up_grad = jnp.sum(pre_gelu_grad, axis=sum_axes, dtype=jnp.float32)
    return source_grad, inward_grad, outward_grad, up_grad, down_grad, early, late, bias_up_grad


def dot(left, right):
    return jnp.dot(left, right, preferred_element_type=jnp.float32)


def dot_back(left, right):
    return lax.dot_general(
        left, right, (((1,), (1,)), ((), ())), preferred_element_type=jnp.float32
    )


def dot_weight(left, right):
    return lax.dot_general(
        left, right, (((0,), (0,)), ((), ())), preferred_element_type=jnp.float32
    )


def cross_forward(inputs, weights, same_document, mine):
    project_in, project_out, up_weight, down_weight, norm_gains, biases, up_bias = weights
    rows, length, features = inputs.shape
    flat = inputs.reshape(rows * length, features)
    source = flat.astype(jnp.bfloat16)
    zeros = jnp.zeros((features,), jnp.float32)
    joined_bias = jnp.concatenate([biases[:, 0], zeros, biases[:, 1]])
    joined = (dot(source, project_in) + mine(joined_bias)).astype(jnp.bfloat16)
    joined = lax.all_gather(joined, "seg", axis=1, tiled=True).reshape(rows, length, -1)
    queries = joined[..., :features]
    key_rows = joined[..., features : 2 * features]
    values = joined[..., 2 * features :]
    head_shape = (rows, length, HEADS, HD)
    scores = soft_scores(queries.reshape(head_shape), key_rows.reshape(head_shape), same_document)
    log_total = jax.nn.logsumexp(scores, axis=-1, keepdims=True)
    attention = jnp.exp(scores - log_total).astype(jnp.bfloat16)
    context = jnp.einsum(
        "ghqk,gkhe->gqhe", attention, values.reshape(head_shape), preferred_element_type=jnp.float32
    )
    context = context.reshape(flat.shape).astype(jnp.bfloat16)
    mixed = lax.all_gather(dot(context, project_out), "seg", axis=1, tiled=True)
    mixed_input = flat + (mixed + biases[:, 2])
    first_norm = norm_apply(mixed_input, norm_gains[:, 0], biases[:, 4])
    first_low = first_norm.astype(jnp.bfloat16)
    pre_gelu = dot(first_low, up_weight) + mine(up_bias)
    activation = gelu_exact(pre_gelu).astype(jnp.bfloat16)
    activation = lax.all_gather(activation, "seg", axis=1, tiled=True)
    branch = lax.all_gather(dot(activation, down_weight), "seg", axis=1, tiled=True)
    second_input = first_norm + (branch + biases[:, 3])
    result = norm_apply(second_input, norm_gains[:, 1], biases[:, 5]).reshape(inputs.shape)
    stored = (
        source,
        queries,
        key_rows,
        values,
        log_total,
        context,
        mixed_input,
        first_low,
        pre_gelu,
        activation,
        second_input,
    )
    return result, stored


def cross_backward(stored, weights, same_document, upstream, mine):
    project_in, project_out, up_weight, down_weight, norm_gains, biases, up_bias = weights
    (
        source,
        queries,
        key_rows,
        values,
        log_total,
        context,
        mixed_input,
        first_low,
        pre_gelu,
        activation,
        second_input,
    ) = stored
    features = source.shape[-1]
    second_grad, gain_two, shift_two = norm_backward(
        second_input, norm_gains[:, 1], biases[:, 5], upstream.reshape(source.shape)
    )
    branch_grad = second_grad.astype(jnp.bfloat16)
    branch_mine = mine(branch_grad)
    down_grad = dot_weight(activation, branch_mine)
    partial = dot_back(branch_mine, down_weight)
    seg = lax.axis_size("seg")
    partial = partial.reshape(partial.shape[0], seg, -1).transpose(1, 0, 2)
    partial = lax.all_to_all(partial, "seg", split_axis=0, concat_axis=0, tiled=True)
    activation_grad = jnp.sum(partial, axis=0)
    unused_out, gelu_pull = jax.vjp(gelu_exact, pre_gelu)
    pre_gelu_grad = gelu_pull(activation_grad)[0].astype(jnp.bfloat16)
    up_grad = dot_weight(first_low, pre_gelu_grad)
    first_grad = second_grad + total_over(dot_back(pre_gelu_grad, up_weight), "seg")
    mixed_grad, gain_one, shift_one = norm_backward(
        mixed_input, norm_gains[:, 0], biases[:, 4], first_grad
    )
    mixed_low = mixed_grad.astype(jnp.bfloat16)
    mixed_mine = mine(mixed_low)
    outward_grad = dot_weight(context, mixed_mine)
    context_grad = total_over(dot_back(mixed_mine, project_out), "seg").astype(jnp.bfloat16)
    joined_grad = attention_backward(
        queries, key_rows, values, log_total, same_document, context_grad.reshape(queries.shape)
    ).reshape(source.shape[0], -1)
    joined_mine = mine(joined_grad)
    inward_grad = dot_weight(source, joined_mine)
    source_grad = mixed_grad + total_over(dot_back(joined_mine, project_in), "seg")
    sums = jnp.sum(joined_grad, axis=0, dtype=jnp.float32)
    bias_grad = jnp.stack(
        [
            sums[:features],
            sums[2 * features :],
            jnp.sum(mixed_low, axis=0, dtype=jnp.float32),
            jnp.sum(branch_grad, axis=0, dtype=jnp.float32),
            shift_one,
            shift_two,
            gain_one,
            gain_two,
        ],
        axis=-1,
    )
    bias_up_grad = jnp.sum(pre_gelu_grad, axis=0, dtype=jnp.float32)
    return (
        source_grad.reshape(upstream.shape),
        (inward_grad, outward_grad, up_grad, down_grad),
        bias_grad,
        bias_up_grad,
    )


def pack_rows(pieces, rows):
    return jnp.concatenate([piece.reshape(rows, -1) for piece in pieces], axis=1)


def gather_local(pieces):
    joined = jnp.concatenate(pieces, axis=1)
    full = lax.all_gather(joined, ("seg", "dp"), axis=0, tiled=False)
    return full.reshape(lax.axis_size("seg"), -1, joined.shape[1])


def unfold(part):
    return part.transpose(1, 0, 2).reshape(part.shape[1], -1)


def reduce_rows(array):
    return lax.psum_scatter(array.astype(jnp.bfloat16), "dp", scatter_dimension=0, tiled=True)


def reduce_columns(array):
    return lax.psum_scatter(array, "seg", scatter_dimension=1, tiled=True).astype(jnp.float32)


def shards(
    tokens,
    cotangent,
    document_ids,
    position_ids,
    project_in,
    project_out,
    up_weight,
    down_weight,
    norm_gains,
    biases,
    up_bias,
    position_table,
):
    shard_index = lax.axis_index("seg")
    seg = lax.axis_size("seg")
    micro_count, row_count, row_tokens, features = tokens.shape
    segment_count = row_tokens // SEGLEN
    rows = micro_count * row_count
    group_count = rows * segment_count
    own_rows = project_in.shape[1]
    wide, out_wide, up_wide = project_in.shape[2], project_out.shape[2], up_weight.shape[2]
    slot_ids = jnp.arange(POS, dtype=jnp.int32)

    def mine(array):
        width = array.shape[-1] // seg
        return lax.dynamic_slice_in_dim(array, shard_index * width, width, array.ndim - 1)

    up_packed = up_bias.reshape(2, own_rows, -1).transpose(1, 0, 2).reshape(own_rows, -1)
    many = up_packed.shape[1] // 2
    small = pack_rows(
        [norm_gains.transpose(1, 0, 2), biases.transpose(1, 0, 2), up_packed, position_table],
        own_rows,
    )
    small = lax.all_gather(small, "dp", axis=0, tiled=True)
    gains_full = small[:, :4].reshape(features, 2, 2).astype(jnp.float32)
    biases_full = small[:, 4:16].reshape(features, 2, 6).astype(jnp.float32)
    up_full = small[:, 16 : 16 + 2 * many].reshape(features, 2, -1).astype(jnp.float32)
    gathered_table = small[:, 16 + 2 * many :]

    def vectors(which):
        return gains_full[:, which], biases_full[:, which], up_full[:, which].reshape(-1)

    attend_full = gather_local([project_in[0], project_out[0]])
    feed_full = gather_local([up_weight[0], down_weight[0].reshape(own_rows, -1)])
    local_weights = (
        unfold(attend_full[:, :, :wide]),
        unfold(attend_full[:, :, wide:]),
        unfold(feed_full[:, :, :up_wide]),
        unfold(feed_full[:, :, up_wide:].reshape(seg, -1, down_weight.shape[2])),
    ) + vectors(0)
    cross_full = lax.all_gather(
        pack_rows([project_in[1], project_out[1], up_weight[1], down_weight[1]], own_rows),
        "dp",
        axis=0,
        tiled=True,
    )
    ends = [wide, wide + out_wide, wide + out_wide + up_wide]
    cross_weights = (
        cross_full[:, : ends[0]],
        cross_full[:, ends[0] : ends[1]],
        cross_full[:, ends[1] : ends[2]],
        cross_full[:, ends[2] :].reshape(-1, down_weight.shape[2]),
    ) + vectors(1)

    segments = tokens.reshape(group_count, SEGLEN, features)
    local_out, local_stored = block_forward(
        segments, segments.astype(jnp.float32), local_weights, None
    )
    class_own = local_out[:, 0, :].astype(jnp.bfloat16).reshape(rows, segment_count, features)
    upstream = cotangent.reshape(group_count, SEGLEN, features)
    class_grad_own = upstream[:, 0, :].reshape(rows, segment_count, features)
    class_grads = lax.all_gather(class_grad_own, "seg", axis=1, tiled=True)
    class_rows = lax.all_gather(class_own, "seg", axis=1, tiled=True)
    positions = position_ids.reshape(rows, -1)
    one_hot = (positions[:, :, None] == slot_ids).astype(jnp.bfloat16)
    cross_in = class_rows.astype(jnp.float32) + jnp.einsum(
        "rsp,dp->rsd", one_hot, gathered_table, preferred_element_type=jnp.float32
    )
    documents = document_ids.reshape(rows, -1)
    same_document = documents[:, :, None] == documents[:, None, :]
    cross_out, cross_stored = cross_forward(cross_in, cross_weights, same_document, mine)
    cross_own = lax.dynamic_slice_in_dim(cross_out, shard_index * segment_count, segment_count, 1)
    merged = local_out.at[:, 0, :].set(cross_own.reshape(group_count, features))
    layer_out = merged.astype(jnp.bfloat16).reshape(tokens.shape)

    cross_grad, cross_terms, cross_bias, cross_up = cross_backward(
        cross_stored, cross_weights, same_document, class_grads.astype(jnp.float32), mine
    )
    table_grad = jnp.einsum("rsd,rsp->dp", cross_grad, one_hot.astype(jnp.float32), precision=PRECISE)
    own_grad = lax.dynamic_slice_in_dim(cross_grad, shard_index * segment_count, segment_count, 1)
    local_upstream = (
        upstream.astype(jnp.float32).at[:, 0, :].set(own_grad.reshape(group_count, features))
    )
    cross_packed = reduce_rows(
        pack_rows([term.astype(jnp.bfloat16) for term in cross_terms], features)
    ).astype(jnp.float32)
    token_grad, inward, outward, up_grad, down_grad, early, late, local_up = local_backward(
        segments, local_stored, local_weights, local_upstream
    )
    input_grad = token_grad.reshape(tokens.shape)
    cross_parts = (
        cross_packed[:, : ends[0]],
        cross_packed[:, ends[0] : ends[1]],
        cross_packed[:, ends[1] : ends[2]],
        cross_packed[:, ends[2] :].reshape(down_weight.shape[1:]),
    )
    down_part = reduce_columns(reduce_rows(down_grad))
    up_part = reduce_columns(reduce_rows(up_grad))
    first_shard = (shard_index == 0).astype(jnp.float32)
    pieces = [
        early,
        local_up.reshape(features, -1),
        cross_bias * first_shard,
        cross_up_full(cross_up, shard_index, seg).reshape(features, -1),
        table_grad * first_shard,
    ]
    attend_grads = jnp.concatenate([inward, outward, late.astype(jnp.bfloat16)], axis=1)
    small_grads = reduce_rows(jnp.concatenate(pieces, axis=1)).astype(jnp.float32)
    small_grads = total_over(small_grads, "seg")
    attend_grads = reduce_rows(attend_grads)
    edge = 3 * features
    inward_part = reduce_columns(attend_grads[:, :edge])
    outward_part = reduce_columns(attend_grads[:, edge : edge + features])
    late = total_over(attend_grads[:, edge + features :].astype(jnp.float32), "seg")
    matrices = tuple(
        jnp.stack(pair)
        for pair in zip((inward_part, outward_part, up_part, down_part), cross_parts)
    )
    start = 6 + many
    cross_small = small_grads[:, start : start + 8]
    gains = jnp.stack([small_grads[:, 4:6], cross_small[:, 6:8]])
    bias_out = jnp.stack(
        [jnp.concatenate([late, small_grads[:, :4]], axis=1), cross_small[:, :6]]
    )
    ups = jnp.stack(
        [small_grads[:, 6:start], small_grads[:, start + 8 : start + 8 + many]]
    ).reshape(up_bias.shape)
    return (layer_out, input_grad) + matrices + (
        gains,
        bias_out,
        ups,
        small_grads[:, start + 8 + many :],
    )


def cross_up_full(own, shard_index, seg):
    full = jnp.zeros((own.shape[0] * seg,), own.dtype)
    return lax.dynamic_update_slice_in_dim(full, own, shard_index * own.shape[0], 0)


def solution(mesh):
    placed = (
        P(None, "dp", "seg", None),
        P(None, "dp", "seg", None),
        P(None, "dp", None),
        P(None, "dp", None),
        P(None, "dp", "seg"),
        P(None, "dp", "seg"),
        P(None, "dp", "seg"),
        P(None, "dp", "seg"),
        P(None, "dp", None),
        P(None, "dp", None),
        P(None, "dp"),
        P("dp", None),
    )
    return jax.shard_map(
        shards,
        mesh=mesh,
        in_specs=placed,
        out_specs=(
            P(None, "dp", "seg", None),
            P(None, "dp", "seg", None),
            P(None, "dp", "seg"),
            P(None, "dp", "seg"),
            P(None, "dp", "seg"),
            P(None, "dp", "seg"),
            P(None, "dp", None),
            P(None, "dp", None),
            P(None, "dp"),
            P("dp", None),
        ),
        check_vma=False,
    )
```

```python
import functools

import jax
import jax.numpy as jnp
from jax import lax
from jax.experimental import pallas as pl
from jax.experimental.pallas import tpu as pltpu
from jax.sharding import PartitionSpec as P

HEADS = 12
HD = 64
SEGLEN = 128
POS = 64


NORM_EPS = 1e-05
PRECISE = lax.Precision.HIGHEST


def vector_rows(norm_gains, biases):
    return jnp.concatenate([biases, norm_gains], axis=1).T


GRANT = 60 * 1024 * 1024
INV_ROOT_TWO = 0.7071067811865476
INV_ROOT_TAU = 0.3989422804014327


def dot(left, right):
    return lax.dot_general(
        left, right, (((1,), (0,)), ((), ())), preferred_element_type=jnp.float32
    )


def dot_nt(left, right):
    return lax.dot_general(
        left, right, (((1,), (1,)), ((), ())), preferred_element_type=jnp.float32
    )


def dot_tn(left, right):
    return lax.dot_general(
        left, right, (((0,), (0,)), ((), ())), preferred_element_type=jnp.float32
    )


def norm_parts(inputs):
    average = jnp.mean(inputs, axis=-1, keepdims=True)
    centered = inputs - average
    variance = jnp.mean(centered * centered, axis=-1, keepdims=True)
    scale = lax.rsqrt(variance + NORM_EPS)
    return centered * scale, scale


def norm_pull(unit, scale, gain, upstream):
    inner = upstream * gain
    return scale * (
        inner
        - jnp.mean(inner, axis=-1, keepdims=True)
        - unit * jnp.mean(inner * unit, axis=-1, keepdims=True)
    )


def gelu_both(inputs):
    below = 0.5 * (1.0 + lax.erf(inputs * INV_ROOT_TWO))
    density = jnp.exp(-0.5 * inputs * inputs) * INV_ROOT_TAU
    return inputs * below, below + inputs * density


def row_sum(array):
    return jnp.sum(array.astype(jnp.float32), axis=0, keepdims=True)


def unfold_kernel(own_rows, packed_ref, up_ref, down_ref):
    up_wide = up_ref.shape[1]
    up_ref[...] = packed_ref[0, :, :up_wide]
    dp = packed_ref.shape[1] // own_rows
    own = down_ref.shape[1] // dp
    halves = down_ref.shape[0] // own_rows
    for place in range(dp):
        for half in range(halves):
            down_ref[
                half * own_rows : (half + 1) * own_rows, place * own : (place + 1) * own
            ] = packed_ref[
                0,
                place * own_rows : (place + 1) * own_rows,
                up_wide + half * own : up_wide + (half + 1) * own,
            ]


def unfold_feed(packed, own_rows, up_wide, down_wide):
    seg, features, both = packed.shape
    ff = seg * up_wide
    dp = features // own_rows
    own = ff // dp
    halves = down_wide // own_rows
    used = up_wide + halves * own
    if up_wide % 128 or own % 128 or own_rows % 16 or used % 128:
        down = packed[:, :, up_wide:used].reshape(seg, dp, own_rows, halves, own)
        down = down.transpose(0, 3, 2, 1, 4).reshape(features, ff)
        return unfold(packed[:, :, :up_wide]), down
    return pl.pallas_call(
        functools.partial(unfold_kernel, own_rows),
        grid=(seg,),
        in_specs=[pl.BlockSpec((1, features, used), lambda z: (z, 0, 0))],
        out_specs=[
            pl.BlockSpec((features, up_wide), lambda z: (0, z)),
            pl.BlockSpec((down_wide, ff), lambda z: (z, 0)),
        ],
        out_shape=[
            jax.ShapeDtypeStruct((features, ff), jnp.bfloat16),
            jax.ShapeDtypeStruct((features, ff), jnp.bfloat16),
        ],
        compiler_params=pltpu.CompilerParams(vmem_limit_bytes=GRANT),
        cost_estimate=pl.CostEstimate(
            flops=0, bytes_accessed=8 * features * ff, transcendentals=0
        ),
    )(packed)


def feed_kernel(
    mixed_ref, up_ref, down_ref, vec_ref, up_bias_ref, low_ref, act_ref, slope_ref, second_ref, out_ref
):
    unit, unused_scale = norm_parts(mixed_ref[...])
    first = unit * vec_ref[6:7, :] + vec_ref[4:5, :]
    low = first.astype(jnp.bfloat16)
    low_ref[...] = low
    total = first + vec_ref[3:4, :]
    ff = up_ref.shape[1]
    step = ff // 4
    for at in range(0, ff, step):
        pre = dot(low, up_ref[:, at : at + step]) + up_bias_ref[:, at : at + step]
        value, slope = gelu_both(pre)
        value = value.astype(jnp.bfloat16)
        act_ref[:, at : at + step] = value
        slope_ref[:, at : at + step] = slope.astype(jnp.bfloat16)
        total = total + dot_nt(value, down_ref[:, at : at + step])
    second_ref[...] = total
    unit, unused_scale = norm_parts(total)
    out_ref[...] = (unit * vec_ref[7:8, :] + vec_ref[5:6, :]).astype(jnp.bfloat16)


def whole_spec(shape):
    return pl.BlockSpec(shape, lambda *at: (0,) * len(shape), pipeline_mode=pl.Buffered(1))


def feed_forward(mixed, up, down, vec, up_bias):
    rows, features = mixed.shape
    ff = up.shape[1]
    tile = 256
    narrow = pl.BlockSpec((tile, features), lambda i: (i, 0))
    broad = pl.BlockSpec((tile, ff), lambda i: (i, 0))
    low = jnp.bfloat16
    return pl.pallas_call(
        feed_kernel,
        grid=(rows // tile,),
        in_specs=[
            narrow,
            whole_spec(up.shape),
            whole_spec(down.shape),
            whole_spec(vec.shape),
            whole_spec(up_bias.shape),
        ],
        out_specs=[narrow, broad, broad, narrow, narrow],
        out_shape=[
            jax.ShapeDtypeStruct((rows, features), low),
            jax.ShapeDtypeStruct((rows, ff), low),
            jax.ShapeDtypeStruct((rows, ff), low),
            jax.ShapeDtypeStruct((rows, features), jnp.float32),
            jax.ShapeDtypeStruct((rows, features), low),
        ],
        compiler_params=pltpu.CompilerParams(vmem_limit_bytes=GRANT),
        cost_estimate=pl.CostEstimate(
            flops=4 * rows * features * ff,
            bytes_accessed=4 * features * ff + 4 * rows * ff + 12 * rows * features,
            transcendentals=2 * rows * ff,
        ),
    )(mixed, up, down, vec, up_bias)


def cross_kernel(
    in_ref, grad_ref, same_ref, in_weight, out_weight, up_ref, down_ref, vec_ref, up_bias_ref,
    out_ref, source_grad_ref, context_ref, low_ref, act_ref, joined_ref, mixed_ref, pre_ref, branch_ref,
    sums_ref, up_sum_ref,
):
    features = in_ref.shape[1]
    root = HD ** (-0.5)
    inputs = in_ref[...]
    same = same_ref[...] > 0.5
    source = inputs.astype(jnp.bfloat16)
    queries = (dot(source, in_weight[:, :features]) + vec_ref[0:1, :]).astype(jnp.bfloat16)
    key_rows = dot(source, in_weight[:, features : 2 * features]).astype(jnp.bfloat16)
    values = (dot(source, in_weight[:, 2 * features :]) + vec_ref[1:2, :]).astype(jnp.bfloat16)
    two = 2 * HD
    lane = lax.broadcasted_iota(jnp.int32, (inputs.shape[0], two), 1)
    lower = lane < HD
    zero = jnp.zeros((inputs.shape[0], two), jnp.bfloat16)

    def only(half, array):
        return jnp.where(lower, array, zero) if half == 0 else jnp.where(lower, zero, array)

    weights = []
    pieces = []
    for at in range(0, features, two):
        pair = []
        for half in range(2):
            scores = dot_nt(only(half, queries[:, at : at + two]), key_rows[:, at : at + two]) * root
            scores = jnp.where(same, scores, -1e30)
            top = jnp.max(scores, axis=-1, keepdims=True)
            log_total = top + jnp.log(jnp.sum(jnp.exp(scores - top), axis=-1, keepdims=True))
            attention = jnp.exp(scores - log_total)
            weights.append(attention)
            pair.append(dot(attention.astype(jnp.bfloat16), values[:, at : at + two]))
        pieces.append(jnp.where(lower, pair[0], pair[1]).astype(jnp.bfloat16))
    context = jnp.concatenate(pieces, axis=1)
    context_ref[...] = context
    mixed = inputs + (dot(context, out_weight[...]) + vec_ref[2:3, :])
    unit_one, scale_one = norm_parts(mixed)
    first = unit_one * vec_ref[6:7, :] + vec_ref[4:5, :]
    low = first.astype(jnp.bfloat16)
    low_ref[...] = low
    ff = up_ref.shape[1]
    step = ff // 4
    slopes = []
    branch = None
    for at in range(0, ff, step):
        pre = dot(low, up_ref[:, at : at + step]) + up_bias_ref[:, at : at + step]
        value, slope = gelu_both(pre)
        slopes.append(slope)
        value = value.astype(jnp.bfloat16)
        act_ref[:, at : at + step] = value
        part = dot_nt(value, down_ref[:, at : at + step])
        branch = part if branch is None else branch + part
    unit_two, scale_two = norm_parts(first + (branch + vec_ref[3:4, :]))
    out_ref[...] = unit_two * vec_ref[7:8, :] + vec_ref[5:6, :]

    upstream = grad_ref[...]
    second_grad = norm_pull(unit_two, scale_two, vec_ref[7:8, :], upstream)
    sums_ref[5:6, :] = row_sum(upstream)
    sums_ref[7:8, :] = row_sum(upstream * unit_two)
    branch_grad = second_grad.astype(jnp.bfloat16)
    branch_ref[...] = branch_grad
    sums_ref[3:4, :] = row_sum(branch_grad)
    first_grad = second_grad
    for number, at in enumerate(range(0, ff, step)):
        part = dot(branch_grad, down_ref[:, at : at + step]) * slopes[number]
        part = part.astype(jnp.bfloat16)
        pre_ref[:, at : at + step] = part
        up_sum_ref[:, at : at + step] = row_sum(part)
        first_grad = first_grad + dot_nt(part, up_ref[:, at : at + step])
    mixed_grad = norm_pull(unit_one, scale_one, vec_ref[6:7, :], first_grad)
    sums_ref[4:5, :] = row_sum(first_grad)
    sums_ref[6:7, :] = row_sum(first_grad * unit_one)
    mixed_low = mixed_grad.astype(jnp.bfloat16)
    mixed_ref[...] = mixed_low
    sums_ref[2:3, :] = row_sum(mixed_low)
    context_grad = dot_nt(mixed_low, out_weight[...]).astype(jnp.bfloat16)
    for number, at in enumerate(range(0, features, two)):
        query_pair, key_pair, value_pair = [], [], []
        for half in range(2):
            attention = weights[2 * number + half]
            pulled = context_grad[:, at : at + two]
            value_pair.append(dot_tn(attention.astype(jnp.bfloat16), pulled))
            soft = dot_nt(only(half, pulled), values[:, at : at + two])
            score = attention * (soft - jnp.sum(soft * attention, axis=-1, keepdims=True))
            score = score.astype(jnp.bfloat16)
            query_pair.append(dot(score, key_rows[:, at : at + two]) * root)
            key_pair.append(dot_tn(score, queries[:, at : at + two]) * root)
        for base, pair in ((0, query_pair), (features, key_pair), (2 * features, value_pair)):
            joined_ref[:, base + at : base + at + two] = jnp.where(lower, pair[0], pair[1]).astype(
                jnp.bfloat16
            )
    joined = joined_ref[...]
    sums_ref[0:1, :] = row_sum(joined[:, :features])
    sums_ref[1:2, :] = row_sum(joined[:, 2 * features :])
    source_grad_ref[...] = mixed_grad + dot_nt(joined, in_weight[...])


def cross_block(inputs, upstream, same, weights, vec, up_bias):
    rows, features = inputs.shape
    ff = up_bias.shape[1]
    wide, low = jnp.float32, jnp.bfloat16
    operands = (inputs, upstream, same) + weights + (vec, up_bias)
    shapes = [
        ((rows, features), wide),
        ((rows, features), wide),
        ((rows, features), low),
        ((rows, features), low),
        ((rows, ff), low),
        ((rows, 3 * features), low),
        ((rows, features), low),
        ((rows, ff), low),
        ((rows, features), low),
        ((8, features), wide),
        ((1, ff), wide),
    ]
    return pl.pallas_call(
        cross_kernel,
        in_specs=[pl.BlockSpec(memory_space=pltpu.VMEM)] * len(operands),
        out_specs=[pl.BlockSpec(memory_space=pltpu.VMEM)] * len(shapes),
        out_shape=[jax.ShapeDtypeStruct(*shape) for shape in shapes],
        compiler_params=pltpu.CompilerParams(vmem_limit_bytes=GRANT),
        cost_estimate=pl.CostEstimate(
            flops=12 * rows * features * (2 * features + ff),
            bytes_accessed=4 * features * (2 * features + ff),
            transcendentals=3 * rows * ff,
        ),
    )(*operands)


def after(value, *earlier):
    return lax.optimization_barrier((value,) + earlier)


def total_over(array, axis_name):
    return jnp.sum(lax.all_gather(array, axis_name, axis=0, tiled=False), axis=0)


def attend_forward_kernel(token_ref, in_weight, out_weight, vec_ref, joined_ref, context_ref, total_ref, mixed_ref):
    rows, features = token_ref.shape
    root = HD ** (-0.5)
    low = jnp.bfloat16
    two = 2 * HD
    source = token_ref[...]
    joined_ref[:, :features] = (dot(source, in_weight[:, :features]) + vec_ref[0:1, :]).astype(low)
    joined_ref[:, features : 2 * features] = dot(source, in_weight[:, features : 2 * features]).astype(low)
    joined_ref[:, 2 * features :] = (dot(source, in_weight[:, 2 * features :]) + vec_ref[1:2, :]).astype(low)
    lane = lax.broadcasted_iota(jnp.int32, (SEGLEN, two), 1)
    lower = lane < HD
    zero = jnp.zeros((SEGLEN, two), low)
    for start in range(0, rows, SEGLEN):
        span = slice(start, start + SEGLEN)
        totals = jnp.zeros((SEGLEN, two), jnp.float32)
        for at in range(0, features, two):
            queries = joined_ref[span, at : at + two]
            key_rows = joined_ref[span, features + at : features + at + two]
            values = joined_ref[span, 2 * features + at : 2 * features + at + two]
            pair = []
            for half in range(2):
                kept = jnp.where(lower, queries, zero) if half == 0 else jnp.where(lower, zero, queries)
                scores = dot_nt(kept, key_rows) * root
                top = jnp.max(scores, axis=-1, keepdims=True)
                log_total = top + jnp.log(jnp.sum(jnp.exp(scores - top), axis=-1, keepdims=True))
                totals = jnp.where(lane == at // HD + half, log_total, totals)
                pair.append(dot(jnp.exp(scores - log_total).astype(low), values))
            context_ref[span, at : at + two] = jnp.where(lower, pair[0], pair[1]).astype(low)
        total_ref[span, :] = totals
    mixed_ref[...] = source.astype(jnp.float32) + (dot(context_ref[...], out_weight[...]) + vec_ref[2:3, :])


def row_blocks(tile, width):
    return pl.BlockSpec((tile, width), lambda i: (i, 0))


def attend_forward(tokens, in_weight, out_weight, vec):
    rows, features = tokens.shape
    tile = 2 * SEGLEN
    low, wide = jnp.bfloat16, jnp.float32
    outs = [(3 * features, low), (features, low), (2 * HD, wide), (features, wide)]
    return pl.pallas_call(
        attend_forward_kernel,
        grid=(rows // tile,),
        in_specs=[
            row_blocks(tile, features),
            whole_spec(in_weight.shape),
            whole_spec(out_weight.shape),
            whole_spec(vec.shape),
        ],
        out_specs=[row_blocks(tile, width) for width, unused_kind in outs],
        out_shape=[jax.ShapeDtypeStruct((rows, width), kind) for width, kind in outs],
        compiler_params=pltpu.CompilerParams(vmem_limit_bytes=GRANT),
        cost_estimate=pl.CostEstimate(
            flops=12 * rows * features * features,
            bytes_accessed=14 * rows * features + 8 * features * features,
            transcendentals=2 * rows * HEADS * SEGLEN,
        ),
    )(tokens, in_weight, out_weight, vec)


def feed_backward_kernel(
    grad_ref, second_ref, mixed_ref, slope_ref, up_ref, down_ref, vec_ref,
    branch_ref, pre_ref, mixed_grad_ref, sums_ref, up_sum_ref,
):
    @pl.when(pl.program_id(0) == 0)
    def clear():
        sums_ref[...] = jnp.zeros_like(sums_ref)
        up_sum_ref[...] = jnp.zeros_like(up_sum_ref)

    upstream = grad_ref[...].astype(jnp.float32)
    unit, scale = norm_parts(second_ref[...])
    second_grad = norm_pull(unit, scale, vec_ref[7:8, :], upstream)
    sums_ref[5:6, :] += row_sum(upstream)
    sums_ref[7:8, :] += row_sum(upstream * unit)
    branch_grad = second_grad.astype(jnp.bfloat16)
    branch_ref[...] = branch_grad
    sums_ref[3:4, :] += row_sum(branch_grad)
    first_grad = second_grad
    ff = up_ref.shape[1]
    step = ff // 4
    for at in range(0, ff, step):
        part = dot(branch_grad, down_ref[:, at : at + step]) * slope_ref[:, at : at + step].astype(jnp.float32)
        part = part.astype(jnp.bfloat16)
        pre_ref[:, at : at + step] = part
        up_sum_ref[:, at : at + step] += row_sum(part)
        first_grad = first_grad + dot_nt(part, up_ref[:, at : at + step])
    unit, scale = norm_parts(mixed_ref[...])
    mixed_grad_ref[...] = norm_pull(unit, scale, vec_ref[6:7, :], first_grad)
    sums_ref[4:5, :] += row_sum(first_grad)
    sums_ref[6:7, :] += row_sum(first_grad * unit)


def feed_backward(upstream, second, mixed, slope, up, down, vec, tile):
    rows, features = mixed.shape
    ff = up.shape[1]
    low, wide = jnp.bfloat16, jnp.float32
    narrow, broad = row_blocks(tile, features), row_blocks(tile, ff)
    return pl.pallas_call(
        feed_backward_kernel,
        grid=(rows // tile,),
        in_specs=[narrow, narrow, narrow, broad]
        + [whole_spec(array.shape) for array in (up, down, vec)],
        out_specs=[
            narrow,
            broad,
            narrow,
            pl.BlockSpec((8, features), lambda i: (0, 0)),
            pl.BlockSpec((1, ff), lambda i: (0, 0)),
        ],
        out_shape=[
            jax.ShapeDtypeStruct((rows, features), low),
            jax.ShapeDtypeStruct((rows, ff), low),
            jax.ShapeDtypeStruct((rows, features), wide),
            jax.ShapeDtypeStruct((8, features), wide),
            jax.ShapeDtypeStruct((1, ff), wide),
        ],
        compiler_params=pltpu.CompilerParams(vmem_limit_bytes=GRANT),
        cost_estimate=pl.CostEstimate(
            flops=4 * rows * features * ff,
            bytes_accessed=4 * features * ff + 4 * rows * ff + 16 * rows * features,
            transcendentals=0,
        ),
    )(upstream, second, mixed, slope, up, down, vec)


def attend_backward_kernel(
    joined_ref, total_ref, mixed_ref, patch_ref, in_weight, out_weight,
    grad_ref, low_ref, source_grad_ref, sums_ref, context_scratch,
):
    step = pl.program_id(0)

    @pl.when(step == 0)
    def clear():
        sums_ref[...] = jnp.zeros_like(sums_ref)

    rows, features = mixed_ref.shape
    root = HD ** (-0.5)
    low = jnp.bfloat16
    two = 2 * HD
    count = rows // SEGLEN
    first_row = lax.broadcasted_iota(jnp.int32, (SEGLEN, features), 0) == 0
    for number in range(count):
        span = slice(number * SEGLEN, (number + 1) * SEGLEN)
        patch = patch_ref[pl.ds(step * count + number, 1), :]
        source_grad_ref[span, :] = jnp.where(first_row, patch, mixed_ref[span, :])
    mixed_low = source_grad_ref[...].astype(low)
    low_ref[...] = mixed_low
    sums_ref[2:3, :] += row_sum(mixed_low)
    context_scratch[...] = dot_nt(mixed_low, out_weight[...]).astype(low)
    lane = lax.broadcasted_iota(jnp.int32, (SEGLEN, two), 1)
    lower = lane < HD
    zero = jnp.zeros((SEGLEN, two), low)
    for number in range(count):
        span = slice(number * SEGLEN, (number + 1) * SEGLEN)
        for at in range(0, features, two):
            queries = joined_ref[span, at : at + two]
            key_rows = joined_ref[span, features + at : features + at + two]
            values = joined_ref[span, 2 * features + at : 2 * features + at + two]
            pulled = context_scratch[span, at : at + two]
            query_pair, key_pair, value_pair = [], [], []
            for half in range(2):
                place = at // HD + half
                if half == 0:
                    kept, some = jnp.where(lower, queries, zero), jnp.where(lower, pulled, zero)
                else:
                    kept, some = jnp.where(lower, zero, queries), jnp.where(lower, zero, pulled)
                scores = dot_nt(kept, key_rows) * root
                attention = jnp.exp(scores - total_ref[span, place : place + 1])
                value_pair.append(dot_tn(attention.astype(low), pulled))
                soft = dot_nt(some, values)
                score = attention * (soft - jnp.sum(soft * attention, axis=-1, keepdims=True))
                score = score.astype(low)
                query_pair.append(dot(score, key_rows))
                key_pair.append(dot_tn(score, queries))
            grad_ref[span, at : at + two] = (jnp.where(lower, *query_pair) * root).astype(low)
            grad_ref[span, features + at : features + at + two] = (
                jnp.where(lower, *key_pair) * root
            ).astype(low)
            grad_ref[span, 2 * features + at : 2 * features + at + two] = jnp.where(
                lower, *value_pair
            ).astype(low)
    sums_ref[0:1, :] += row_sum(grad_ref[:, :features])
    sums_ref[1:2, :] += row_sum(grad_ref[:, 2 * features :])
    source_grad_ref[...] += dot_nt(grad_ref[...], in_weight[...])


def attend_backward(joined, totals, mixed_grad, patch, in_weight, out_weight):
    rows, features = mixed_grad.shape
    tile = 2 * SEGLEN
    low, wide = jnp.bfloat16, jnp.float32
    narrow, broad = row_blocks(tile, features), row_blocks(tile, 3 * features)
    return pl.pallas_call(
        attend_backward_kernel,
        grid=(rows // tile,),
        in_specs=[
            broad,
            row_blocks(tile, 2 * HD),
            narrow,
            whole_spec(patch.shape),
            whole_spec(in_weight.shape),
            whole_spec(out_weight.shape),
        ],
        out_specs=[broad, narrow, narrow, pl.BlockSpec((8, features), lambda i: (0, 0))],
        out_shape=[
            jax.ShapeDtypeStruct((rows, 3 * features), low),
            jax.ShapeDtypeStruct((rows, features), low),
            jax.ShapeDtypeStruct((rows, features), wide),
            jax.ShapeDtypeStruct((8, features), wide),
        ],
        scratch_shapes=[pltpu.VMEM((tile, features), low)],
        compiler_params=pltpu.CompilerParams(vmem_limit_bytes=GRANT),
        cost_estimate=pl.CostEstimate(
            flops=14 * rows * features * features,
            bytes_accessed=20 * rows * features + 8 * features * features,
            transcendentals=rows * HEADS * SEGLEN,
        ),
    )(joined, totals, mixed_grad, patch, in_weight, out_weight)


def pack_rows(pieces, rows):
    return jnp.concatenate([piece.reshape(rows, -1) for piece in pieces], axis=1)


def gather_local(pieces):
    joined = jnp.concatenate(pieces, axis=1)
    full = lax.all_gather(joined, ("seg", "dp"), axis=0, tiled=False)
    return full.reshape(lax.axis_size("seg"), -1, joined.shape[1])


def unfold(part):
    return part.transpose(1, 0, 2).reshape(part.shape[1], -1)


def reduce_rows(array, earlier):
    array = array.astype(jnp.bfloat16)
    if earlier is not None:
        array = after(array, earlier)[0]
    return lax.psum_scatter(array, "dp", scatter_dimension=0, tiled=True)


def reduce_columns(arrays, earlier):
    seg = lax.axis_size("seg")
    blocks = jnp.concatenate(
        [array.reshape(array.shape[0], seg, -1).transpose(1, 0, 2) for array in arrays], axis=2
    )
    blocks = after(blocks, earlier)[0]
    return lax.psum_scatter(blocks, "seg", scatter_dimension=0, tiled=True)[0].astype(jnp.float32)


def shards(
    tokens,
    cotangent,
    document_ids,
    position_ids,
    project_in,
    project_out,
    up_weight,
    down_weight,
    norm_gains,
    biases,
    up_bias,
    position_table,
):
    shard_index = lax.axis_index("seg")
    seg = lax.axis_size("seg")
    micro_count, row_count, row_tokens, features = tokens.shape
    segment_count = row_tokens // SEGLEN
    rows = micro_count * row_count
    group_count = rows * segment_count
    own_rows = project_in.shape[1]
    wide, out_wide, up_wide = project_in.shape[2], project_out.shape[2], up_weight.shape[2]
    slot_ids = jnp.arange(POS, dtype=jnp.int32)

    def mine(array):
        width = array.shape[-1] // seg
        return lax.dynamic_slice_in_dim(array, shard_index * width, width, array.ndim - 1)

    up_packed = up_bias.reshape(2, own_rows, -1).transpose(1, 0, 2).reshape(own_rows, -1)
    many = up_packed.shape[1] // 2
    small = pack_rows(
        [norm_gains.transpose(1, 0, 2), biases.transpose(1, 0, 2), up_packed, position_table],
        own_rows,
    )
    small = lax.all_gather(small, "dp", axis=0, tiled=True)
    gains_full = small[:, :4].reshape(features, 2, 2).astype(jnp.float32)
    biases_full = small[:, 4:16].reshape(features, 2, 6).astype(jnp.float32)
    up_full = small[:, 16 : 16 + 2 * many].reshape(features, 2, -1).astype(jnp.float32)
    gathered_table = small[:, 16 + 2 * many :]

    def vectors(which):
        return gains_full[:, which], biases_full[:, which], up_full[:, which].reshape(-1)

    down_wide = down_weight.shape[2]

    def turned(which):
        own = down_weight[which].T.reshape(-1, own_rows, down_weight.shape[1])
        return own.transpose(1, 0, 2).reshape(own_rows, -1)

    attend_full = gather_local([project_in[0], project_out[0]])
    feed_full = gather_local([up_weight[0], turned(0)])
    local_weights = (
        unfold(attend_full[:, :, :wide]),
        unfold(attend_full[:, :, wide:]),
        *unfold_feed(feed_full, own_rows, up_wide, down_wide),
    ) + vectors(0)
    cross_full = gather_local(
        [up_weight[1], turned(1), project_in[1], project_out[1]]
    )
    upstream = cotangent.reshape(group_count, SEGLEN, features)
    class_grad_own = upstream[:, 0, :].reshape(rows, segment_count, features)
    class_grads = lax.all_gather(class_grad_own, "seg", axis=1, tiled=True)
    flat = tokens.reshape(-1, features)
    in_weight, out_weight, up_full_local, down_full_local, gains, shifts, up_shift = local_weights
    local_vec = vector_rows(gains, shifts)
    joined, context_local, log_totals, mixed = attend_forward(flat, in_weight, out_weight, local_vec)
    first_low_local, act_local, slope, second, local_out = feed_forward(
        mixed, up_full_local, down_full_local, local_vec, up_shift[None]
    )
    local_out = local_out.reshape(upstream.shape)
    first_token = (jnp.arange(SEGLEN) == 0)[None, :, None]
    others = jnp.where(first_token, jnp.zeros((), upstream.dtype), upstream)
    branch_local, pre_local, mixed_grad, feed_sums, up_sums = feed_backward(
        others.reshape(-1, features),
        second,
        mixed,
        slope,
        up_full_local,
        down_full_local,
        local_vec,
        256,
    )
    cross_full = after(cross_full, mixed_grad)[0]
    cross_weights = (
        unfold(cross_full[:, :, 2 * up_wide : 2 * up_wide + wide]),
        unfold(cross_full[:, :, 2 * up_wide + wide :]),
        *unfold_feed(cross_full, own_rows, up_wide, down_wide),
    )
    class_own = local_out[:, 0, :].reshape(rows, segment_count, features)
    class_rows = lax.all_gather(class_own, "seg", axis=1, tiled=True)
    positions = position_ids.reshape(rows, -1)
    one_hot = (positions[:, :, None] == slot_ids).astype(jnp.bfloat16)
    cross_in = class_rows.astype(jnp.float32) + jnp.einsum(
        "rsp,dp->rsd", one_hot, gathered_table, preferred_element_type=jnp.float32
    )
    documents = document_ids.reshape(rows, -1)
    length = documents.shape[1]
    same_document = documents[:, :, None] == documents[:, None, :]
    same = jnp.where(jnp.eye(rows, dtype=bool)[:, None, :, None], same_document[:, :, None, :], False)
    gains, shifts, up_shift = vectors(1)
    (
        cross_out,
        cross_grad,
        context,
        first_low,
        activation,
        joined_grad,
        mixed_low,
        pre_gelu_grad,
        branch_grad,
        cross_sums,
        cross_up_sum,
    ) = cross_block(
        cross_in.reshape(-1, features),
        class_grads.astype(jnp.float32).reshape(-1, features),
        same.reshape(rows * length, rows * length).astype(jnp.float32),
        cross_weights,
        vector_rows(gains, shifts),
        up_shift[None],
    )
    cross_source = cross_in.astype(jnp.bfloat16).reshape(-1, features)
    cross_out = cross_out.reshape(rows, length, features)
    cross_grad = cross_grad.reshape(rows, length, features)
    cross_own = lax.dynamic_slice_in_dim(cross_out, shard_index * segment_count, segment_count, 1)
    merged = local_out.at[:, 0, :].set(
        cross_own.reshape(group_count, features).astype(jnp.bfloat16)
    )
    layer_out = merged.reshape(tokens.shape)
    cross_terms = [
        dot_tn(cross_source, mine(joined_grad)),
        dot_tn(context, mine(mixed_low)),
        dot_tn(first_low, mine(pre_gelu_grad)),
        dot_tn(activation, mine(branch_grad)),
    ]
    table_grad = jnp.einsum("rsd,rsp->dp", cross_grad, one_hot.astype(jnp.float32), precision=PRECISE)
    own_grad = lax.dynamic_slice_in_dim(cross_grad, shard_index * segment_count, segment_count, 1)
    cross_packed = pack_rows([term.astype(jnp.bfloat16) for term in cross_terms], features)
    own_grad, cross_packed = after(own_grad, cross_packed)
    cross_packed = reduce_rows(cross_packed, None)

    def class_of(array):
        return array.reshape(group_count, SEGLEN, -1)[:, 0, :]

    def with_class(array, patch):
        shape = array.shape
        array = array.reshape(group_count, SEGLEN, -1)
        return lax.dynamic_update_slice(array, patch[:, None, :], (0, 0, 0)).reshape(shape)

    class_branch, class_pre, class_mixed, class_sums, class_up_sums = feed_backward(
        own_grad.reshape(group_count, features),
        class_of(second),
        class_of(mixed),
        class_of(slope),
        up_full_local,
        down_full_local,
        local_vec,
        group_count,
    )
    feed_sums = feed_sums + class_sums
    up_sums = up_sums + class_up_sums
    down_grad = dot_tn(act_local, with_class(branch_local, class_branch)).astype(jnp.bfloat16)
    pre_local = with_class(pre_local, class_pre)
    pre_local, down_grad = after(pre_local, down_grad)
    up_grad = dot_tn(first_low_local, pre_local).astype(jnp.bfloat16)
    class_mixed, up_grad = after(class_mixed, up_grad)
    joined_local, mixed_low_local, token_grad, attend_sums = attend_backward(
        joined, log_totals, mixed_grad, class_mixed, in_weight, out_weight
    )
    outward = dot_tn(context_local, mixed_low_local).astype(jnp.bfloat16)
    inward = dot_tn(flat, joined_local).astype(jnp.bfloat16)
    input_grad = token_grad.reshape(tokens.shape)
    down_rows_sum = reduce_rows(down_grad, cross_packed)
    up_rows_sum = reduce_rows(up_grad, down_rows_sum)
    first_shard = (shard_index == 0).astype(jnp.float32)
    local_sums = jnp.concatenate([attend_sums[:3], feed_sums[3:]], axis=0)
    pieces = [
        local_sums.T,
        up_sums.reshape(features, -1),
        cross_sums.T * first_shard,
        cross_up_sum.reshape(features, -1) * first_shard,
        table_grad * first_shard,
    ]
    small_grads = reduce_rows(jnp.concatenate(pieces, axis=1), up_rows_sum)
    attend_rows = reduce_rows(jnp.concatenate([inward, outward], axis=1), small_grads)
    small_grads = total_over(small_grads.astype(jnp.float32), "seg")
    edge = 3 * features
    block_part = reduce_columns(
        [
            attend_rows[:, :edge],
            attend_rows[:, edge:],
            up_rows_sum,
            down_rows_sum.reshape(own_rows, -1, seg, down_wide)
            .transpose(0, 2, 1, 3)
            .reshape(own_rows, -1),
        ],
        attend_rows,
    )
    down_packed = down_weight.shape[1:]
    ends = [wide, wide + out_wide, wide + out_wide + up_wide]
    cross_packed = cross_packed.astype(jnp.float32)
    matrices = (
        jnp.stack([block_part[:, : ends[0]], cross_packed[:, : ends[0]]]),
        jnp.stack([block_part[:, ends[0] : ends[1]], cross_packed[:, ends[0] : ends[1]]]),
        jnp.stack([block_part[:, ends[1] : ends[2]], cross_packed[:, ends[1] : ends[2]]]),
        jnp.stack(
            [
                block_part[:, ends[2] :].reshape(down_packed),
                cross_packed[:, ends[2] :].reshape(down_packed),
            ]
        ),
    )
    start = 8 + many
    gains = jnp.stack([small_grads[:, 6:8], small_grads[:, start + 6 : start + 8]])
    bias_out = jnp.stack([small_grads[:, :6], small_grads[:, start : start + 6]])
    ups = jnp.stack(
        [small_grads[:, 8:start], small_grads[:, start + 8 : start + 8 + many]]
    ).reshape(up_bias.shape)
    return (layer_out, input_grad) + matrices + (
        gains,
        bias_out,
        ups,
        small_grads[:, start + 8 + many :],
    )


def solution(mesh):
    placed = (
        P(None, "dp", "seg", None),
        P(None, "dp", "seg", None),
        P(None, "dp", None),
        P(None, "dp", None),
        P(None, "dp", "seg"),
        P(None, "dp", "seg"),
        P(None, "dp", "seg"),
        P(None, "dp", "seg"),
        P(None, "dp", None),
        P(None, "dp", None),
        P(None, "dp"),
        P("dp", None),
    )
    return jax.shard_map(
        shards,
        mesh=mesh,
        in_specs=placed,
        out_specs=(
            P(None, "dp", "seg", None),
            P(None, "dp", "seg", None),
            P(None, "dp", "seg"),
            P(None, "dp", "seg"),
            P(None, "dp", "seg"),
            P(None, "dp", "seg"),
            P(None, "dp", None),
            P(None, "dp", None),
            P(None, "dp"),
            P("dp", None),
        ),
        check_vma=False,
    )
```
